32 devices in a mesh: gx: 8 (over z, core), gy: 4 (over y, x).
Axes of the slice: x: 2, y: 2, z: 4, core: 2. Of those that a mesh axis runs over, the one named last changes fastest.
Arguments:
- tracers: bfloat16 [8, 64, 32, 256], P(None, 'gx', 'gy'), may hold values from -6 to 6
- velocity: float32 [2, 64, 32], P(None, 'gx', 'gy'), may hold values from -0.04 to 0.04
- inflow: int32 [4, 64, 32], P(None, 'gx', 'gy'), may hold values from 0 to 1, as said below
- leaf_solve: float32 [256, 256], replicated, may hold values from -0.375 to 0.375
- leaf_skeleton: float32 [256, 64], replicated, may hold values from -0.375 to 0.375
- leaf_lift: float32 [64, 256], replicated, may hold values from -0.75 to 0.75
- merge_first: float32 [128, 64], replicated, may hold values from -0.5 to 0.5
- merge_second: float32 [128, 128], replicated, may hold values from -0.5 to 0.5
- merge_rest: float32 [9, 256, 128], replicated, may hold values from -0.375 to 0.375
- parent_first: float32 [64, 128], replicated, may hold values from -0.75 to 0.75
- parent_second: float32 [128, 128], replicated, may hold values from -0.5 to 0.5
- parent_rest: float32 [9, 128, 256], replicated, may hold values from -0.5 to 0.5
- sibling_first: float32 [128, 128], replicated, may hold values from -0.125 to 0.125
- sibling_second: float32 [128, 128], replicated, may hold values from -0.125 to 0.125
- sibling_rest: float32 [9, 256, 256], replicated, may hold values from -0.09375 to 0.09375
- root_map: float32 [128, 128], replicated, may hold values from -0.5 to 0.5
Outputs:
- updated: bfloat16 [8, 64, 32, 256], P(None, 'gx', 'gy')
The draws below stay inside these ranges and needn't reach their ends.
Inputs may be any that keep to these rules, and one draw needn't show every extreme that they name: inflow[0] of leaf (i, j) equals 1 minus inflow[1] of leaf (i - 1, j), and inflow[2] of leaf (i, j) equals 1 minus inflow[3] of leaf (i, j - 1); inflow[1] is 0 on the last leaves along the first dimension and inflow[3] on the last leaves along the second.
All inputs are finite; a program needn't handle non-finite values.
Results may differ from the reference program's by a relative error of at most 0.001.
Values may be sent and summed in bfloat16 or wider, within the bound.
A program may use at most 64 MiB of HBM per device.

```python
import jax
import jax.numpy as jnp
from jax import lax

TRACERS = 8
NODE = 16
NODES = 256
LEAF_SKEL = 64
RANK = 128
LEAF_SIDE = 8
LEAVES_X = 64
LEAVES_Y = 32
LEVELS = 11
N_GX = 8
N_GY = 4


def draw_inflow(key, part):
    key_first, key_second = jax.random.split(jax.random.fold_in(key, 11))
    low_first = jax.random.randint(key_first, (LEAVES_X, LEAVES_Y), 0, 2, dtype=jnp.int32)
    low_second = jax.random.randint(key_second, (LEAVES_X, LEAVES_Y), 0, 2, dtype=jnp.int32)
    high_first = jnp.concatenate([1 - low_first[1:], jnp.zeros((1, LEAVES_Y), jnp.int32)], axis=0)
    high_second = jnp.concatenate([1 - low_second[:, 1:], jnp.zeros((LEAVES_X, 1), jnp.int32)], axis=1)
    return jnp.stack([low_first, high_first, low_second, high_second]).astype(jnp.int32)


def shard_levels(key, extent, shards, least, top_value):
    level = 1.0
    for dim, blocks in shards:
        heights = jax.random.uniform(jax.random.fold_in(jax.random.fold_in(key, 6), dim), (blocks,), jnp.float32, least / len(shards), top_value / len(shards))
        level = level * jnp.repeat(jnp.exp(heights), extent[dim] // blocks).reshape((-1,) + (1,) * (len(extent) - 1 - dim))
    return level


def normal_values(stream_key, dims, deviation, most, cuts=(), held_as=jnp.bfloat16):
    result = jax.random.normal(stream_key, dims, jnp.float32) * deviation
    if len(cuts) > 0:
        result = shard_levels(stream_key, dims, cuts, -0.22, 0.18) * result
    return jnp.clip(result, min=-most, max=most).astype(held_as)


def setup_inputs(seed: int = 0) -> dict:
    seeds = jax.random.split(jax.random.key(seed), 17)
    return {
        "tracers": normal_values(seeds[0], (TRACERS, LEAVES_X, LEAVES_Y, NODES), 1.0, 6.0, ((1, 8), (2, 4))),
        "velocity": jnp.clip(jax.random.uniform(seeds[1], (2, LEAVES_X, LEAVES_Y), jnp.float32, -0.04, 0.04) * shard_levels(seeds[1], (2, LEAVES_X, LEAVES_Y), ((1, 8), (2, 4)), -0.4, 0.0), -0.04, 0.04),
        "inflow": draw_inflow(jax.random.fold_in(seeds[16], 71), 0),
        "leaf_solve": normal_values(seeds[3], (NODES, NODES), NODES ** -0.5, 0.375, (), jnp.float32),
        "leaf_skeleton": normal_values(seeds[4], (NODES, LEAF_SKEL), NODES ** -0.5, 0.375, (), jnp.float32),
        "leaf_lift": normal_values(seeds[5], (LEAF_SKEL, NODES), LEAF_SKEL ** -0.5, 0.75, (), jnp.float32),
        "merge_first": normal_values(seeds[6], (2 * LEAF_SKEL, LEAF_SKEL), (2 * LEAF_SKEL) ** -0.5, 0.5, (), jnp.float32),
        "merge_second": normal_values(seeds[7], (2 * LEAF_SKEL, RANK), (2 * LEAF_SKEL) ** -0.5, 0.5, (), jnp.float32),
        "merge_rest": normal_values(seeds[8], (LEVELS - 2, 2 * RANK, RANK), (2 * RANK) ** -0.5, 0.375, (), jnp.float32),
        "parent_first": normal_values(seeds[9], (LEAF_SKEL, 2 * LEAF_SKEL), LEAF_SKEL ** -0.5, 0.75, (), jnp.float32),
        "parent_second": normal_values(seeds[10], (RANK, 2 * LEAF_SKEL), RANK ** -0.5, 0.5, (), jnp.float32),
        "parent_rest": normal_values(seeds[11], (LEVELS - 2, RANK, 2 * RANK), RANK ** -0.5, 0.5, (), jnp.float32),
        "sibling_first": normal_values(seeds[12], (2 * LEAF_SKEL, 2 * LEAF_SKEL), (32 * LEAF_SKEL) ** -0.5, 0.125, (), jnp.float32),
        "sibling_second": normal_values(seeds[13], (2 * LEAF_SKEL, 2 * LEAF_SKEL), (32 * LEAF_SKEL) ** -0.5, 0.125, (), jnp.float32),
        "sibling_rest": normal_values(seeds[14], (LEVELS - 2, 2 * RANK, 2 * RANK), (32 * RANK) ** -0.5, 0.09375, (), jnp.float32),
        "root_map": normal_values(seeds[15], (RANK, RANK), RANK ** -0.5, 0.5, (), jnp.float32),
    }


highest = lax.Precision.HIGHEST


def product(left, right):
    return jnp.dot(left, right, precision=highest, preferred_element_type=jnp.float32)


def spectral_matrix(node_count):
    node_index = jnp.arange(node_count)
    points = -jnp.cos(jnp.pi * node_index.astype(jnp.float32) / (node_count - 1))
    end_weights = jnp.where((node_index == 0) | (node_index == node_count - 1), 2.0, 1.0)
    parity = jnp.where(node_index % 2 == 0, 1.0, -1.0)
    weights = (end_weights * parity).astype(jnp.float32)
    identity = jnp.eye(node_count, dtype=jnp.float32)
    offsets = points[:, None] - points[None, :] + identity
    matrix = (weights[:, None] / weights[None, :]) / offsets * (1.0 - identity)
    return matrix - jnp.diag(jnp.sum(matrix, axis=1))


def derivative_tables(node_count):
    spectral = spectral_matrix(node_count)
    identity = jnp.eye(node_count, dtype=jnp.float32)
    return jnp.concatenate([jnp.kron(spectral, identity).T, jnp.kron(identity, spectral).T], axis=1)


def side_table(node_count):
    node_index = jnp.arange(node_count * node_count)
    along_first = node_index // node_count
    along_second = node_index % node_count
    position = jnp.arange(node_count)[:, None]
    table_rows = [(along_first[None, :] == 0) & (along_second[None, :] == position),
                  (along_first[None, :] == node_count - 1) & (along_second[None, :] == position),
                  (along_second[None, :] == 0) & (along_first[None, :] == position),
                  (along_second[None, :] == node_count - 1) & (along_first[None, :] == position)]
    return jnp.concatenate(table_rows, axis=0).astype(jnp.float32)


def edge_values(tracer_field, node_count):
    node_grid = tracer_field.reshape(tracer_field.shape[:-1] + (node_count, node_count))
    return (node_grid[..., 0, :], node_grid[..., node_count - 1, :],
            node_grid[..., :, 0], node_grid[..., :, node_count - 1])


def forcing_term(tracer_field, own_edges, neighbours, velocity, inflow):
    node_count = own_edges[0].shape[-1]
    square = node_count * node_count
    gradients = product(tracer_field, derivative_tables(node_count))
    advective = velocity[0][None, :, :, None] * gradients[..., :square] + velocity[1][None, :, :, None] * gradients[..., square:]
    penalty_terms = []
    for side_index in range(4):
        strength = inflow[side_index].astype(jnp.float32) * (node_count * jnp.abs(velocity[side_index // 2]))
        penalty_terms.append(strength[None, :, :, None] * (neighbours[side_index] - own_edges[side_index]))
    penalty = product(jnp.concatenate(penalty_terms, axis=-1), side_table(node_count))
    return tracer_field - advective + penalty


def level_operators(level, tables):
    if level == 0:
        return tables[0]
    if level == 1:
        return tables[1]
    return tuple(stacked[level - 2] for stacked in tables[2])


def split_pairs(current, merge_axis):
    new_shape = current.shape[:merge_axis] + (current.shape[merge_axis] // 2, 2) + current.shape[merge_axis + 1:]
    paired = current.reshape(new_shape)
    return lax.index_in_dim(paired, 0, merge_axis + 1, False), lax.index_in_dim(paired, 1, merge_axis + 1, False)


def join_pairs(former, latter, merge_axis):
    joined = jnp.stack([former, latter], axis=merge_axis + 1)
    new_shape = list(former.shape)
    new_shape[merge_axis] = new_shape[merge_axis] * 2
    return joined.reshape(tuple(new_shape))


def ascend(current, merge_plan, start_level, tables):
    levels = []
    for offset, merge_axis in enumerate(merge_plan):
        level = start_level + offset
        former, latter = split_pairs(current, merge_axis)
        levels.append((former, latter, merge_axis, level))
        current = product(jnp.concatenate([former, latter], axis=-1), level_operators(level, tables)[0])
    return current, levels


def descend(boundary, levels, tables):
    for former, latter, merge_axis, level in reversed(levels):
        operators = level_operators(level, tables)
        joined_pair = product(boundary, operators[1]) + product(
            jnp.concatenate([former, latter], axis=-1), operators[2])
        half_width = joined_pair.shape[-1] // 2
        boundary = join_pairs(joined_pair[..., :half_width], joined_pair[..., half_width:], merge_axis)
    return boundary


def local_plan(leaf_side):
    merge_plan = []
    block_span = leaf_side
    while block_span > 1:
        merge_plan = merge_plan + [1, 2]
        block_span = block_span // 2
    return merge_plan


def cross_plan(count_first, count_second):
    merge_plan = []
    while count_first * count_second > 1:
        if count_first >= count_second:
            merge_plan.append(1)
            count_first = count_first // 2
        else:
            merge_plan.append(2)
            count_second = count_second // 2
    return merge_plan


def reference(tracers, velocity, inflow, leaf_solve, leaf_skeleton, leaf_lift, merge_first, merge_second, merge_rest,
              parent_first, parent_second, parent_rest, sibling_first, sibling_second, sibling_rest, root_map):
    merge_plan = local_plan(LEAF_SIDE) + cross_plan(N_GX, N_GY)
    tables = ((merge_first, parent_first, sibling_first), (merge_second, parent_second, sibling_second),
              (merge_rest, parent_rest, sibling_rest))

    def one_tracer(tracer_slice):
        tracer_field = tracer_slice.astype(jnp.float32)[None]
        own_edges = edge_values(tracer_field, NODE)
        zeros_first = jnp.zeros_like(own_edges[0][:, :1])
        zeros_second = jnp.zeros_like(own_edges[2][:, :, :1])
        neighbours = (jnp.concatenate([zeros_first, own_edges[1][:, :-1]], axis=1),
                      jnp.concatenate([own_edges[0][:, 1:], zeros_first], axis=1),
                      jnp.concatenate([zeros_second, own_edges[3][:, :, :-1]], axis=2),
                      jnp.concatenate([own_edges[2][:, :, 1:], zeros_second], axis=2))
        forcing = forcing_term(tracer_field, own_edges, neighbours, velocity, inflow)
        skeleton = product(forcing, leaf_skeleton)
        tree_root, levels = ascend(skeleton, merge_plan, 0, tables)
        leaf_boundary = descend(product(tree_root, root_map), levels, tables)
        updated = product(forcing, leaf_solve) + product(leaf_boundary, leaf_lift)
        return updated.astype(jnp.bfloat16)[0]

    return lax.map(one_tracer, tracers)
```

```python
import functools

import jax
import jax.numpy as jnp
import numpy as np
from jax import lax
from jax.experimental import pallas as pl
from jax.experimental.pallas import tpu as pltpu
from jax.sharding import PartitionSpec as P

NODE = 16
SQUARE = NODE * NODE
F32 = jnp.float32
BF16 = jnp.bfloat16
MESH = pl.DeviceIdType.MESH


def local_plan(leaf_side):
    merge_plan = []
    block_span = leaf_side
    while block_span > 1:
        merge_plan = merge_plan + [1, 2]
        block_span = block_span // 2
    return merge_plan


def cross_plan(count_first, count_second):
    merge_plan = []
    bits = {"gx": 0, "gy": 0}
    while count_first * count_second > 1:
        if count_first >= count_second:
            axis, count_first = "gx", count_first // 2
        else:
            axis, count_second = "gy", count_second // 2
        merge_plan.append((axis, bits[axis]))
        bits[axis] += 1
    return merge_plan


def staged(plan):
    stages, start, size = [], 0, 2
    while start < len(plan):
        stages.append(plan[start : start + size])
        start, size = start + size, 3
    return stages


def point_tables():
    index = np.arange(NODE)
    points = -np.cos(np.pi * index / (NODE - 1))
    weights = np.where(index % 2 == 0, 1.0, -1.0)
    weights[[0, NODE - 1]] *= 2.0
    eye = np.eye(NODE)
    matrix = weights[:, None] / weights[None, :] / (points[:, None] - points[None, :] + eye)
    matrix = matrix * (1.0 - eye)
    matrix = matrix - np.diag(matrix.sum(axis=1))
    both = np.concatenate([np.kron(matrix, eye).T, np.kron(eye, matrix).T], axis=1)
    both = both.astype(np.float32)
    high = both.astype(jnp.bfloat16)
    low = (both - high.astype(np.float32)).astype(jnp.bfloat16)
    facing = np.zeros((SQUARE, 2 * SQUARE), np.float32)
    last = NODE - 1
    for k in range(NODE):
        facing[last * NODE + k, k] = 1.0
        facing[k, last * NODE + k] = 1.0
        facing[k * NODE + last, SQUARE + k * NODE] = 1.0
        facing[k * NODE, SQUARE + k * NODE + last] = 1.0
    return np.concatenate([high, low, facing.astype(jnp.bfloat16)], axis=1)


def split(x):
    high = x.astype(BF16)
    return high, (x - high.astype(F32)).astype(BF16)


def dot(left, right):
    return jnp.dot(left, right, preferred_element_type=F32)


def product(x, weight):
    high, low = weight
    rows = x.shape[0]
    if rows >= 64:
        x_high, x_low = split(x)
        return dot(x_high, high) + dot(x_low, high) + dot(x_high, low)
    rest = x - x.astype(BF16).astype(F32)
    both = jnp.concatenate([x, rest], axis=0).astype(BF16)
    out = dot(both, high) + dot(both, low)
    return out[:rows] + out[rows:]


def lanes(shape):
    return lax.broadcasted_iota(jnp.int32, shape, len(shape) - 1)


def left_half(shape):
    return lanes(shape) < shape[-1] // 2


def kernel(stages, leaf_side, tracer_count, *refs):
    names = ["u", "velocity", "inflow", "tables", "leaf_solve", "leaf_skeleton", "leaf_lift"]
    names += [a + "_" + b for a in ("merge", "parent", "sibling") for b in ("first", "second", "rest")]
    names += ["root_map"]
    hbm = dict(zip(names, refs[: len(names)]))
    out_ref = refs[len(names)]
    rest = refs[len(names) + 1 :]
    v = dict(zip(names, rest[: len(names)]))
    (
        load_sem, force, near, w_second, level_one, down_one, solved, t0_ref, t1_ref,
        up_high, up_low, par_high, par_low,
        send_x, send_y, halo_x, halo_y, halo_send, halo_recv,
    ) = rest[len(names) : len(names) + 19]
    stage_refs = rest[len(names) + 19 :]
    T, L = tracer_count, leaf_side
    leaves = L * L
    rows = T * leaves

    loads = {}
    for k, name in enumerate(names):
        loads[name] = pltpu.make_async_copy(hbm[name], v[name], load_sem.at[k])
    order = ["u", "tables", "velocity", "inflow", "leaf_skeleton"]
    order += ["merge_first", "merge_second", "merge_rest", "leaf_solve"]
    order += ["sibling_first", "sibling_second", "sibling_rest", "parent_rest", "root_map"]
    order += ["parent_second", "parent_first", "leaf_lift"]
    for name in order:
        loads[name].start()

    place = {"gx": lax.axis_index("gx"), "gy": lax.axis_index("gy")}
    count = {"gx": lax.axis_size("gx"), "gy": lax.axis_size("gy")}
    bit_of = lambda axis, bit: lax.rem(place[axis] // (1 << bit), 2)

    def partner(stage, mask):
        target = dict(place)
        for k, (axis, bit) in enumerate(stage):
            if mask >> (len(stage) - 1 - k) & 1:
                target[axis] = target[axis] + (1 - 2 * bit_of(axis, bit)) * (1 << bit)
        return (target["gx"], target["gy"])

    barrier = pltpu.get_barrier_semaphore()
    expected = jnp.int32(0)
    for stage in stages:
        for mask in range(1, 1 << len(stage)):
            pl.semaphore_signal(barrier, inc=1, device_id=partner(stage, mask), device_id_type=MESH)
            expected = expected + 1
    has, beside = {}, {}
    for axis in ("gx", "gy"):
        for way in (-1, 1):
            spot = dict(place)
            spot[axis] = spot[axis] + way
            beside[axis, way] = (spot["gx"], spot["gy"])
            has[axis, way] = place[axis] > 0 if way < 0 else place[axis] < count[axis] - 1

            @pl.when(has[axis, way])
            def _(axis=axis, way=way):
                pl.semaphore_signal(barrier, inc=1, device_id=beside[axis, way], device_id_type=MESH)

            expected = expected + jnp.where(has[axis, way], 1, 0)

    loads["u"].wait()
    loads["tables"].wait()
    u = v["u"][...].astype(F32).reshape(rows, SQUARE)
    ub = u.astype(BF16)
    facing = dot(ub, v["tables"][:, 4 * SQUARE :])
    for c in range(4):
        near[c * rows : (c + 1) * rows, :] = facing[:, c * 128 : (c + 1) * 128]
    for t in range(T):
        base = t * leaves
        send_x[1, t * L : (t + 1) * L, :] = facing[base + leaves - L : base + leaves, :128]
        send_x[0, t * L : (t + 1) * L, :] = facing[base : base + L, 128:256]
    for k in range(2):
        for c in range(2):
            line = pl.ds((2 + c) * rows + k * (L - 1), T * L, stride=L)
            send_y[k, c * T * L : (c + 1) * T * L, :] = near[line, :]
    pl.semaphore_wait(barrier, expected)

    def halo_copy(axis, way):
        k = 0 if way < 0 else 1
        source, target = (send_x, halo_x) if axis == "gx" else (send_y, halo_y)
        slot = k + (0 if axis == "gx" else 2)
        return pltpu.make_async_remote_copy(
            src_ref=source.at[k],
            dst_ref=target.at[k],
            send_sem=halo_send.at[slot],
            recv_sem=halo_recv.at[slot],
            device_id=beside[axis, way],
            device_id_type=MESH,
        )

    sides = [("gy", -1), ("gy", 1), ("gx", -1), ("gx", 1)]
    for axis, way in sides:

        @pl.when(has[axis, way])
        def _(axis=axis, way=way):
            halo_copy(axis, way).start()

    loads["velocity"].wait()
    loads["inflow"].wait()
    own = lax.broadcasted_iota(jnp.int32, (leaves, L), 0) % L == lanes((leaves, L))

    def column(grid):
        wide = jnp.concatenate(
            [jnp.broadcast_to(grid[i : i + 1, :], (L, L)) for i in range(L)], axis=0
        )
        return jnp.sum(jnp.where(own, wide, 0.0), axis=1, keepdims=True)

    speed = [v["velocity"][k] for k in range(2)]
    strength = [
        column(v["inflow"][s].astype(F32) * (NODE * jnp.abs(speed[s // 2]))) for s in range(4)
    ]
    half = (leaves, SQUARE // 2)
    full = (leaves, SQUARE)
    weight_0 = jnp.where(lanes(half) < NODE, strength[0], 0.0)
    weight_1 = jnp.where(lanes(half) >= SQUARE // 2 - NODE, strength[1], 0.0)
    weight_2 = jnp.where(lanes(full) % NODE == 0, strength[2], 0.0)
    weight_3 = jnp.where(lanes(full) % NODE == NODE - 1, strength[3], 0.0)
    for k, weight in enumerate((weight_2, weight_3)):
        for c in range(2):
            at = (2 * k + c) * leaves
            w_second[at : at + leaves, :] = weight[:, c * 128 : (c + 1) * 128]
    keep = 1.0 - (jnp.concatenate([weight_0, weight_1], axis=1) + weight_2 + weight_3)
    spot = lax.broadcasted_iota(jnp.int32, full, 0) % L
    inner_2 = jnp.where(spot == 0, 0.0, weight_2)
    inner_3 = jnp.where(spot == L - 1, 0.0, weight_3)
    speed_0, speed_1 = column(speed[0]), column(speed[1])
    grads = dot(ub, v["tables"][:, : 2 * SQUARE]) + dot(ub, v["tables"][:, 2 * SQUARE : 4 * SQUARE])
    empty = jnp.zeros((L, SQUARE // 2), F32)
    for t in range(T):
        low, top = t * leaves, (t + 1) * leaves
        own_u = u[low:top]
        own_first = facing[low:top, :SQUARE]
        own_second = facing[low:top, SQUARE:].reshape(L, L, SQUARE)
        from_0 = jnp.concatenate([empty, own_first[: leaves - L, : SQUARE // 2]], axis=0)
        from_1 = jnp.concatenate([own_first[L:, SQUARE // 2 :], empty], axis=0)
        from_2 = pltpu.roll(own_second, 1, 1).reshape(leaves, SQUARE)
        from_3 = pltpu.roll(own_second, L - 1, 1).reshape(leaves, SQUARE)
        first = jnp.concatenate([weight_0 * from_0, weight_1 * from_1], axis=1)
        total = (
            keep * own_u
            - speed_0 * grads[low:top, :SQUARE]
            - speed_1 * grads[low:top, SQUARE:]
            + first
            + inner_2 * from_2
            + inner_3 * from_3
        )
        for c in range(2):
            force[c * rows + low : c * rows + top, :] = total[:, c * 128 : (c + 1) * 128]

    for name in ("leaf_skeleton", "merge_first", "merge_second", "merge_rest"):
        loads[name].wait()
    depth = v["merge_rest"].shape[0]
    for k in range(depth):
        up_high[k], up_low[k] = split(v["merge_rest"][k])
    up = lambda k: (up_high[k], up_low[k])
    twice = lambda w, axis: jnp.concatenate([w, w], axis=axis)
    w_skeleton = split(twice(v["leaf_skeleton"][...], 1))
    w_first = split(twice(v["merge_first"][...], 1))
    w_merge_second = split(v["merge_second"][...])

    for axis, way in sides:

        @pl.when(has[axis, way])
        def _(axis=axis, way=way):
            k = 0 if way < 0 else 1
            halo_copy(axis, way).wait_send()
            halo_copy(axis, -way).wait_recv()
            arrived = (halo_x if axis == "gx" else halo_y)[1 - k]
            if axis == "gx":
                edge = 0 if way < 0 else leaves - L
                weight = weight_0[:L] if way < 0 else weight_1[leaves - L :]
                for t in range(T):
                    start = k * rows + t * leaves + edge
                    at = slice(start, start + L)
                    force[at, :] = force[at, :] + weight * arrived[t * L : (t + 1) * L]
            else:
                edge = 0 if way < 0 else L - 1
                for c in range(2):
                    weight = w_second[pl.ds((2 * k + c) * leaves + edge, L, stride=L), :]
                    weight = jnp.concatenate([weight] * T, axis=0)
                    at = pl.ds(c * rows + edge, T * L, stride=L)
                    line = arrived[c * T * L : (c + 1) * T * L]
                    force[at, :] = force[at, :] + weight * line

    forcing = jnp.concatenate([force[:rows, :], force[rows:, :]], axis=1)
    skeleton = product(forcing, w_skeleton).reshape(T, L // 2, 2, L, 128)
    pair = (T * leaves // 2, 128)
    cat_0 = jnp.where(
        left_half(pair), skeleton[:, :, 0].reshape(pair), skeleton[:, :, 1].reshape(pair)
    )
    level_one[...] = product(cat_0, w_first)
    boxes = [
        (a + 2 * c, b + 2 * d) for a in range(2) for b in range(2) for c in range(2) for d in range(2)
    ]
    stride = leaves // 2
    at_box = lambda i, j: pl.ds(i * L + j, T, stride=stride)
    is_left = left_half((T, 128))
    cat_1 = jnp.concatenate(
        [
            jnp.where(is_left, level_one[at_box(i, 2 * j), :], level_one[at_box(i, 2 * j + 1), :])
            for i, j in boxes
        ],
        axis=0,
    )
    current = product(cat_1, w_merge_second)

    def joined(x):
        middle = x.shape[0] // 2
        return jnp.concatenate([x[:middle], x[middle:]], axis=1)

    cats = []
    for k in range(4):
        cats.append(joined(current))
        current = product(cats[-1], up(k))

    level = 4
    path = []
    for number, stage in enumerate(stages):
        pool, stage_send, stage_recv = stage_refs[3 * number : 3 * number + 3]
        slots = 1 << len(stage)
        own_slot = jnp.int32(0)
        for axis, bit in stage:
            own_slot = own_slot * 2 + bit_of(axis, bit)
        pool[own_slot] = current
        copies = [
            pltpu.make_async_remote_copy(
                src_ref=pool.at[own_slot],
                dst_ref=pool.at[own_slot],
                send_sem=stage_send.at[mask],
                recv_sem=stage_recv.at[mask],
                device_id=partner(stage, mask),
                device_id_type=MESH,
            )
            for mask in range(1, slots)
        ]
        for copy in reversed(copies):
            copy.start()
        if number == 0:
            for name in ("leaf_solve", "sibling_first", "sibling_second", "sibling_rest"):
                loads[name].wait()
            local_terms = [product(cats[k], split(v["sibling_rest"][k])) for k in range(4)]
            t1_ref[...] = product(cat_1, split(v["sibling_second"][...]))
            t0_ref[...] = product(cat_0, split(v["sibling_first"][...]))
        if number == len(stages) - 1:
            solved[...] = product(forcing, split(v["leaf_solve"][...]))
            for name in ("parent_rest", "root_map", "parent_second", "parent_first", "leaf_lift"):
                loads[name].wait()
            for k in range(depth):
                par_high[k], par_low[k] = split(v["parent_rest"][k])
            w_root = split(v["root_map"][...])
            w_parent_second = split(v["parent_second"][...])
            w_parent_first = split(twice(v["parent_first"][...], 0))
            w_lift = split(twice(v["leaf_lift"][...], 0))
        for copy in copies:
            copy.wait()
        current = pool[...].reshape(slots * T, 128)
        for k, (axis, bit) in enumerate(stage):
            cat = joined(current)
            mine = cat
            for later_axis, later_bit in stage[k + 1 :]:
                middle = mine.shape[0] // 2
                mine = jnp.where(bit_of(later_axis, later_bit) == 1, mine[middle:], mine[:middle])
            path.append((level, bit_of(axis, bit), product(mine, split(v["sibling_rest"][level]))))
            current = product(cat, up(level))
            level += 1

    down = lambda k: (par_high[k], par_low[k])
    boundary = product(current, w_root)
    for level, bit, term in reversed(path):
        both = product(boundary, down(level)) + term
        boundary = jnp.where(bit == 1, both[:, 128:], both[:, :128])
    for k in reversed(range(4)):
        both = product(boundary, down(k)) + local_terms[k]
        boundary = jnp.concatenate([both[:, :128], both[:, 128:]], axis=0)
    both = product(boundary, w_parent_second) + t1_ref[...]
    for k, (i, j) in enumerate(boxes):
        one = both[k * T : (k + 1) * T]
        down_one[at_box(i, 2 * j), :] = jnp.where(is_left, one, 0.0)
        down_one[at_box(i, 2 * j + 1), :] = jnp.where(is_left, 0.0, one)
    both = product(down_one[...], w_parent_first) + t0_ref[...]
    split_left = left_half(pair)
    shape = (T, L // 2, 1, L, 128)
    leaf_boundary = jnp.concatenate(
        [
            jnp.where(split_left, both, 0.0).reshape(shape),
            jnp.where(split_left, 0.0, both).reshape(shape),
        ],
        axis=2,
    ).reshape(rows, 128)
    updated = solved[...] + product(leaf_boundary, w_lift)
    out_ref[...] = updated.reshape(out_ref.shape).astype(out_ref.dtype)


def local(tables, count_first, count_second, tracers, *operands):
    T, L = tracers.shape[0], tracers.shape[1]
    assert L == 8 and local_plan(L) == [1, 2] * 3
    stages = staged(cross_plan(count_first, count_second))
    rows = T * L * L
    args = (tracers, operands[0], operands[1], tables) + operands[2:]
    depth = operands[7].shape[0]
    vmem, dma = pltpu.VMEM, pltpu.SemaphoreType.DMA
    scratch = [vmem(a.shape, a.dtype) for a in args]
    scratch += [
        dma((len(args),)),
        vmem((2 * rows, 128), F32),
        vmem((4 * rows, 128), F32),
        vmem((4 * L * L, 128), F32),
        vmem((rows // 2, 128), F32),
        vmem((rows // 2, 128), F32),
        vmem((rows, SQUARE), F32),
        vmem((rows // 2, 128), F32),
        vmem((rows // 4, 128), F32),
        vmem((depth, 256, 128), BF16),
        vmem((depth, 256, 128), BF16),
        vmem((depth, 128, 256), BF16),
        vmem((depth, 128, 256), BF16),
        vmem((2, T * L, 128), F32),
        vmem((2, 2 * T * L, 128), F32),
        vmem((2, T * L, 128), F32),
        vmem((2, 2 * T * L, 128), F32),
        dma((4,)),
        dma((4,)),
    ]
    for stage in stages:
        slots = 1 << len(stage)
        scratch += [vmem((slots, T, 128), F32), dma((slots,)), dma((slots,))]
    return pl.pallas_call(
        functools.partial(kernel, stages, L, T),
        out_shape=jax.ShapeDtypeStruct(tracers.shape, tracers.dtype),
        in_specs=[pl.BlockSpec(memory_space=pl.ANY)] * len(args),
        out_specs=pl.BlockSpec(memory_space=pltpu.VMEM),
        scratch_shapes=scratch,
        compiler_params=pltpu.CompilerParams(
            collective_id=0, has_side_effects=True, vmem_limit_bytes=60 * 1024 * 1024
        ),
    )(*args)


def solution(mesh):
    tables = point_tables()
    split_both = P(None, "gx", "gy")
    in_specs = (P(None, "gx", "gy", None), split_both, split_both) + (P(),) * 13

    def body(*args):
        return local(
            jnp.asarray(tables), mesh.shape["gx"], mesh.shape["gy"], *args
        )

    return jax.shard_map(
        body,
        mesh=mesh,
        in_specs=in_specs,
        out_specs=P(None, "gx", "gy", None),
        check_vma=False,
    )
```

```python
import functools

import jax
import jax.numpy as jnp
import numpy as np
from jax import lax
from jax.experimental import pallas as pl
from jax.experimental.pallas import tpu as pltpu
from jax.sharding import PartitionSpec as P

NODE = 16
SQUARE = NODE * NODE
F32 = jnp.float32
BF16 = jnp.bfloat16
VMEM_LIMIT = 60 * 1024 * 1024
MESH = pl.DeviceIdType.MESH


def local_plan(leaf_side):
    merge_plan = []
    block_span = leaf_side
    while block_span > 1:
        merge_plan = merge_plan + [1, 2]
        block_span = block_span // 2
    return merge_plan


def cross_plan(count_first, count_second):
    merge_plan = []
    bits = {"gx": 0, "gy": 0}
    while count_first * count_second > 1:
        if count_first >= count_second:
            axis, count_first = "gx", count_first // 2
        else:
            axis, count_second = "gy", count_second // 2
        merge_plan.append((axis, bits[axis]))
        bits[axis] += 1
    return merge_plan


def staged(plan):
    stages, start, size = [], 0, 2
    while start < len(plan):
        stages.append(plan[start : start + size])
        start, size = start + size, 3
    return stages


def point_tables():
    index = np.arange(NODE)
    points = -np.cos(np.pi * index / (NODE - 1))
    weights = np.where(index % 2 == 0, 1.0, -1.0)
    weights[[0, NODE - 1]] *= 2.0
    eye = np.eye(NODE)
    matrix = weights[:, None] / weights[None, :] / (points[:, None] - points[None, :] + eye)
    matrix = matrix * (1.0 - eye)
    matrix = matrix - np.diag(matrix.sum(axis=1))
    both = np.concatenate([np.kron(matrix, eye).T, np.kron(eye, matrix).T], axis=1)
    both = both.astype(np.float32)
    high = both.astype(jnp.bfloat16)
    low = (both - high.astype(np.float32)).astype(jnp.bfloat16)
    facing = np.zeros((SQUARE, 2 * SQUARE), np.float32)
    last = NODE - 1
    for k in range(NODE):
        facing[last * NODE + k, k] = 1.0
        facing[k, last * NODE + k] = 1.0
        facing[k * NODE + last, SQUARE + k * NODE] = 1.0
        facing[k * NODE, SQUARE + k * NODE + last] = 1.0
    return np.concatenate([high, low, facing.astype(jnp.bfloat16)], axis=1)


def split(x):
    high = x.astype(BF16)
    return high, (x - high.astype(F32)).astype(BF16)


def dot(left, right):
    return jnp.dot(left, right, preferred_element_type=F32)


def dot_across(left, right):
    return lax.dot_general(left, right, (((1,), (1,)), ((), ())), preferred_element_type=F32)


def product(x, weight, dot=dot):
    high, low = weight
    rows = x.shape[0]
    if rows >= 64:
        x_high, x_low = split(x)
        return dot(x_high, high) + dot(x_low, high) + dot(x_high, low)
    rest = x - x.astype(BF16).astype(F32)
    both = jnp.concatenate([x, rest], axis=0).astype(BF16)
    out = dot(both, high) + dot(both, low)
    return out[:rows] + out[rows:]


def lanes(shape):
    return lax.broadcasted_iota(jnp.int32, shape, len(shape) - 1)


def left_half(shape):
    return lanes(shape) < shape[-1] // 2


def kernel(stages, leaf_side, tracer_count, *refs):
    names = ["u", "velocity", "inflow", "tables", "leaf_solve", "leaf_skeleton", "leaf_lift"]
    names += [a + "_" + b for a in ("merge", "parent", "sibling") for b in ("first", "second", "rest")]
    names += ["root_map"]
    hbm = dict(zip(names, refs[: len(names)]))
    out_ref = refs[len(names)]
    rest = refs[len(names) + 1 :]
    v = dict(zip(names, rest[: len(names)]))
    (
        load_sem, force, near, w_second, level_one, down_one, solved, t0_ref, t1_ref,
        up_high, up_low, par_high, par_low,
        send_x, send_y, halo_x, halo_y, halo_send, halo_recv,
    ) = rest[len(names) : len(names) + 19]
    stage_refs = rest[len(names) + 19 :]
    T, L = tracer_count, leaf_side
    leaves = L * L
    rows = T * leaves

    loads = {}
    for k, name in enumerate(names):
        loads[name] = pltpu.make_async_copy(hbm[name], v[name], load_sem.at[k])
    order = ["u", "tables", "velocity", "inflow", "leaf_skeleton"]
    order += ["merge_first", "merge_second", "merge_rest", "leaf_solve"]
    order += ["sibling_first", "sibling_second", "sibling_rest", "parent_rest", "root_map"]
    order += ["parent_second", "parent_first", "leaf_lift"]
    for name in order:
        loads[name].start()

    place = {"gx": lax.axis_index("gx"), "gy": lax.axis_index("gy")}
    count = {"gx": lax.axis_size("gx"), "gy": lax.axis_size("gy")}
    bit_of = lambda axis, bit: lax.rem(place[axis] // (1 << bit), 2)

    def partner(stage, mask):
        target = dict(place)
        for k, (axis, bit) in enumerate(stage):
            if mask >> (len(stage) - 1 - k) & 1:
                target[axis] = target[axis] + (1 - 2 * bit_of(axis, bit)) * (1 << bit)
        return (target["gx"], target["gy"])

    barrier = pltpu.get_barrier_semaphore()
    expected = jnp.int32(0)
    for stage in stages:
        for mask in range(1, 1 << len(stage)):
            pl.semaphore_signal(barrier, inc=1, device_id=partner(stage, mask), device_id_type=MESH)
            expected = expected + 1
    has, beside = {}, {}
    for axis in ("gx", "gy"):
        for way in (-1, 1):
            spot = dict(place)
            spot[axis] = spot[axis] + way
            beside[axis, way] = (spot["gx"], spot["gy"])
            has[axis, way] = place[axis] > 0 if way < 0 else place[axis] < count[axis] - 1

            @pl.when(has[axis, way])
            def _(axis=axis, way=way):
                pl.semaphore_signal(barrier, inc=1, device_id=beside[axis, way], device_id_type=MESH)

            expected = expected + jnp.where(has[axis, way], 1, 0)

    loads["u"].wait()
    loads["tables"].wait()
    u = v["u"][...].astype(F32).reshape(rows, SQUARE)
    ub = u.astype(BF16)
    facing = dot(ub, v["tables"][:, 4 * SQUARE :])
    for c in range(4):
        near[c * rows : (c + 1) * rows, :] = facing[:, c * 128 : (c + 1) * 128]
    for t in range(T):
        base = t * leaves
        send_x[1, t * L : (t + 1) * L, :] = facing[base + leaves - L : base + leaves, :128]
        send_x[0, t * L : (t + 1) * L, :] = facing[base : base + L, 128:256]
    for k in range(2):
        for c in range(2):
            line = pl.ds((2 + c) * rows + k * (L - 1), T * L, stride=L)
            send_y[k, c * T * L : (c + 1) * T * L, :] = near[line, :]
    pl.semaphore_wait(barrier, expected)

    def halo_copy(axis, way):
        k = 0 if way < 0 else 1
        source, target = (send_x, halo_x) if axis == "gx" else (send_y, halo_y)
        slot = k + (0 if axis == "gx" else 2)
        return pltpu.make_async_remote_copy(
            src_ref=source.at[k],
            dst_ref=target.at[k],
            send_sem=halo_send.at[slot],
            recv_sem=halo_recv.at[slot],
            device_id=beside[axis, way],
            device_id_type=MESH,
        )

    sides = [("gy", -1), ("gy", 1), ("gx", -1), ("gx", 1)]
    for axis, way in sides:

        @pl.when(has[axis, way])
        def _(axis=axis, way=way):
            halo_copy(axis, way).start()

    loads["velocity"].wait()
    loads["inflow"].wait()
    own = lax.broadcasted_iota(jnp.int32, (leaves, L), 0) % L == lanes((leaves, L))

    def column(grid):
        wide = jnp.concatenate(
            [jnp.broadcast_to(grid[i : i + 1, :], (L, L)) for i in range(L)], axis=0
        )
        return jnp.sum(jnp.where(own, wide, 0.0), axis=1, keepdims=True)

    speed = [v["velocity"][k] for k in range(2)]
    strength = [
        column(v["inflow"][s].astype(F32) * (NODE * jnp.abs(speed[s // 2]))) for s in range(4)
    ]
    half = (leaves, SQUARE // 2)
    full = (leaves, SQUARE)
    weight_0 = jnp.where(lanes(half) < NODE, strength[0], 0.0)
    weight_1 = jnp.where(lanes(half) >= SQUARE // 2 - NODE, strength[1], 0.0)
    weight_2 = jnp.where(lanes(full) % NODE == 0, strength[2], 0.0)
    weight_3 = jnp.where(lanes(full) % NODE == NODE - 1, strength[3], 0.0)
    for k, weight in enumerate((weight_2, weight_3)):
        for c in range(2):
            at = (2 * k + c) * leaves
            w_second[at : at + leaves, :] = weight[:, c * 128 : (c + 1) * 128]
    keep = 1.0 - (jnp.concatenate([weight_0, weight_1], axis=1) + weight_2 + weight_3)
    spot = lax.broadcasted_iota(jnp.int32, full, 0) % L
    inner_2 = jnp.where(spot == 0, 0.0, weight_2)
    inner_3 = jnp.where(spot == L - 1, 0.0, weight_3)
    speed_0, speed_1 = column(speed[0]), column(speed[1])
    grads = dot(ub, v["tables"][:, : 2 * SQUARE]) + dot(ub, v["tables"][:, 2 * SQUARE : 4 * SQUARE])
    empty = jnp.zeros((L, SQUARE // 2), F32)
    for t in range(T):
        low, top = t * leaves, (t + 1) * leaves
        own_u = u[low:top]
        own_first = facing[low:top, :SQUARE]
        own_second = facing[low:top, SQUARE:].reshape(L, L, SQUARE)
        from_0 = jnp.concatenate([empty, own_first[: leaves - L, : SQUARE // 2]], axis=0)
        from_1 = jnp.concatenate([own_first[L:, SQUARE // 2 :], empty], axis=0)
        from_2 = pltpu.roll(own_second, 1, 1).reshape(leaves, SQUARE)
        from_3 = pltpu.roll(own_second, L - 1, 1).reshape(leaves, SQUARE)
        first = jnp.concatenate([weight_0 * from_0, weight_1 * from_1], axis=1)
        total = (
            keep * own_u
            - speed_0 * grads[low:top, :SQUARE]
            - speed_1 * grads[low:top, SQUARE:]
            + first
            + inner_2 * from_2
            + inner_3 * from_3
        )
        for c in range(2):
            force[c * rows + low : c * rows + top, :] = total[:, c * 128 : (c + 1) * 128]

    for name in ("leaf_skeleton", "merge_first", "merge_second", "merge_rest"):
        loads[name].wait()
    depth = v["merge_rest"].shape[0]
    for k in range(depth):
        up_high[k], up_low[k] = split(v["merge_rest"][k])
    up = lambda k: (up_high[k], up_low[k])
    twice = lambda w, axis: jnp.concatenate([w, w], axis=axis)
    w_skeleton = split(twice(v["leaf_skeleton"][...], 0))
    w_first = split(twice(v["merge_first"][...], 0))
    w_merge_second = split(v["merge_second"][...])

    for axis, way in sides:

        @pl.when(has[axis, way])
        def _(axis=axis, way=way):
            k = 0 if way < 0 else 1
            halo_copy(axis, way).wait_send()
            halo_copy(axis, -way).wait_recv()
            arrived = (halo_x if axis == "gx" else halo_y)[1 - k]
            if axis == "gx":
                edge = 0 if way < 0 else leaves - L
                weight = weight_0[:L] if way < 0 else weight_1[leaves - L :]
                for t in range(T):
                    start = k * rows + t * leaves + edge
                    at = slice(start, start + L)
                    force[at, :] = force[at, :] + weight * arrived[t * L : (t + 1) * L]
            else:
                edge = 0 if way < 0 else L - 1
                for c in range(2):
                    weight = w_second[pl.ds((2 * k + c) * leaves + edge, L, stride=L), :]
                    weight = jnp.concatenate([weight] * T, axis=0)
                    at = pl.ds(c * rows + edge, T * L, stride=L)
                    line = arrived[c * T * L : (c + 1) * T * L]
                    force[at, :] = force[at, :] + weight * line

    forcing = jnp.concatenate([force[:rows, :], force[rows:, :]], axis=1)
    skeleton = product(forcing, w_skeleton, dot_across).reshape(T, L // 2, 2, L, 128)
    pair = (T * leaves // 2, 128)
    cat_0 = jnp.where(
        left_half(pair), skeleton[:, :, 0].reshape(pair), skeleton[:, :, 1].reshape(pair)
    )
    level_one[...] = product(cat_0, w_first, dot_across)
    boxes = [
        (a + 2 * c, b + 2 * d) for a in range(2) for b in range(2) for c in range(2) for d in range(2)
    ]
    stride = leaves // 2
    at_box = lambda i, j: pl.ds(i * L + j, T, stride=stride)
    is_left = left_half((T, 128))
    cat_1 = jnp.concatenate(
        [
            jnp.where(is_left, level_one[at_box(i, 2 * j), :], level_one[at_box(i, 2 * j + 1), :])
            for i, j in boxes
        ],
        axis=0,
    )
    current = product(cat_1, w_merge_second)

    def joined(x):
        middle = x.shape[0] // 2
        return jnp.concatenate([x[:middle], x[middle:]], axis=1)

    cats = []
    for k in range(4):
        cats.append(joined(current))
        current = product(cats[-1], up(k))

    level = 4
    path = []
    for number, stage in enumerate(stages):
        pool, stage_send, stage_recv = stage_refs[3 * number : 3 * number + 3]
        slots = 1 << len(stage)
        own_slot = jnp.int32(0)
        for axis, bit in stage:
            own_slot = own_slot * 2 + bit_of(axis, bit)
        pool[own_slot] = current
        copies = [
            pltpu.make_async_remote_copy(
                src_ref=pool.at[own_slot],
                dst_ref=pool.at[own_slot],
                send_sem=stage_send.at[mask],
                recv_sem=stage_recv.at[mask],
                device_id=partner(stage, mask),
                device_id_type=MESH,
            )
            for mask in range(1, slots)
        ]
        for copy in reversed(copies):
            copy.start()
        if number == 0:
            for name in ("leaf_solve", "sibling_first", "sibling_second", "sibling_rest"):
                loads[name].wait()
            local_terms = [product(cats[k], split(v["sibling_rest"][k])) for k in range(4)]
            t1_ref[...] = product(cat_1, split(v["sibling_second"][...]))
            t0_ref[...] = product(cat_0, split(v["sibling_first"][...]))
        if number == len(stages) - 1:
            solved[...] = product(forcing, split(v["leaf_solve"][...]))
            for name in ("parent_rest", "root_map", "parent_second", "parent_first", "leaf_lift"):
                loads[name].wait()
            for k in range(depth):
                par_high[k], par_low[k] = split(v["parent_rest"][k])
            w_root = split(v["root_map"][...])
            w_parent_second = split(v["parent_second"][...])
            w_parent_first = split(twice(v["parent_first"][...], 0))
            w_lift = split(twice(v["leaf_lift"][...], 0))
        for copy in copies:
            copy.wait()
        current = pool[...].reshape(slots * T, 128)
        for k, (axis, bit) in enumerate(stage):
            cat = joined(current)
            mine = cat
            for later_axis, later_bit in stage[k + 1 :]:
                middle = mine.shape[0] // 2
                mine = jnp.where(bit_of(later_axis, later_bit) == 1, mine[middle:], mine[:middle])
            path.append((level, bit_of(axis, bit), product(mine, split(v["sibling_rest"][level]))))
            current = product(cat, up(level))
            level += 1

    down = lambda k: (par_high[k], par_low[k])
    boundary = product(current, w_root)
    for level, bit, term in reversed(path):
        both = product(boundary, down(level)) + term
        boundary = jnp.where(bit == 1, both[:, 128:], both[:, :128])
    for k in reversed(range(4)):
        both = product(boundary, down(k)) + local_terms[k]
        boundary = jnp.concatenate([both[:, :128], both[:, 128:]], axis=0)
    both = product(boundary, w_parent_second) + t1_ref[...]
    for k, (i, j) in enumerate(boxes):
        one = both[k * T : (k + 1) * T]
        down_one[at_box(i, 2 * j), :] = jnp.where(is_left, one, 0.0)
        down_one[at_box(i, 2 * j + 1), :] = jnp.where(is_left, 0.0, one)
    both = product(down_one[...], w_parent_first) + t0_ref[...]
    split_left = left_half(pair)
    shape = (T, L // 2, 1, L, 128)
    leaf_boundary = jnp.concatenate(
        [
            jnp.where(split_left, both, 0.0).reshape(shape),
            jnp.where(split_left, 0.0, both).reshape(shape),
        ],
        axis=2,
    ).reshape(rows, 128)
    updated = solved[...] + product(leaf_boundary, w_lift)
    out_ref[...] = updated.reshape(out_ref.shape).astype(out_ref.dtype)


def local(tables, count_first, count_second, tracers, *operands):
    T, L = tracers.shape[0], tracers.shape[1]
    assert L == 8 and local_plan(L) == [1, 2] * 3
    stages = staged(cross_plan(count_first, count_second))
    rows = T * L * L
    args = [tracers, operands[0], operands[1], tables] + list(operands[2:])
    args[5], args[7] = args[5].T, args[7].T
    depth = operands[7].shape[0]
    vmem, dma = pltpu.VMEM, pltpu.SemaphoreType.DMA
    scratch = [vmem(a.shape, a.dtype) for a in args]
    scratch += [
        dma((len(args),)),
        vmem((2 * rows, 128), F32),
        vmem((4 * rows, 128), F32),
        vmem((4 * L * L, 128), F32),
        vmem((rows // 2, 128), F32),
        vmem((rows // 2, 128), F32),
        vmem((rows, SQUARE), F32),
        vmem((rows // 2, 128), F32),
        vmem((rows // 4, 128), F32),
        vmem((depth, 256, 128), BF16),
        vmem((depth, 256, 128), BF16),
        vmem((depth, 128, 256), BF16),
        vmem((depth, 128, 256), BF16),
        vmem((2, T * L, 128), F32),
        vmem((2, 2 * T * L, 128), F32),
        vmem((2, T * L, 128), F32),
        vmem((2, 2 * T * L, 128), F32),
        dma((4,)),
        dma((4,)),
    ]
    for stage in stages:
        slots = 1 << len(stage)
        scratch += [vmem((slots, T, 128), F32), dma((slots,)), dma((slots,))]
    return pl.pallas_call(
        functools.partial(kernel, stages, L, T),
        out_shape=jax.ShapeDtypeStruct(tracers.shape, tracers.dtype),
        in_specs=[pl.BlockSpec(memory_space=pl.ANY)] * len(args),
        out_specs=pl.BlockSpec(memory_space=pltpu.VMEM),
        scratch_shapes=scratch,
        compiler_params=pltpu.CompilerParams(
            collective_id=0, has_side_effects=True, vmem_limit_bytes=VMEM_LIMIT
        ),
    )(*args)


def solution(mesh):
    tables = point_tables()
    split_both = P(None, "gx", "gy")
    in_specs = (P(None, "gx", "gy", None), split_both, split_both) + (P(),) * 13

    def body(*args):
        return local(
            jnp.asarray(tables), mesh.shape["gx"], mesh.shape["gy"], *args
        )

    return jax.shard_map(
        body,
        mesh=mesh,
        in_specs=in_specs,
        out_specs=P(None, "gx", "gy", None),
        check_vma=False,
    )
```

```python
import functools

import jax
import jax.numpy as jnp
import numpy as np
from jax import lax
from jax.experimental import pallas as pl
from jax.experimental.pallas import tpu as pltpu
from jax.sharding import PartitionSpec as P

NODE = 16
SQUARE = NODE * NODE
F32 = jnp.float32
BF16 = jnp.bfloat16
VMEM_LIMIT = 32 * 1024 * 1024
MESH = pl.DeviceIdType.MESH


def local_plan(leaf_side):
    merge_plan = []
    block_span = leaf_side
    while block_span > 1:
        merge_plan = merge_plan + [1, 2]
        block_span = block_span // 2
    return merge_plan


def cross_plan(count_first, count_second):
    merge_plan = []
    bits = {"gx": 0, "gy": 0}
    while count_first * count_second > 1:
        if count_first >= count_second:
            axis, count_first = "gx", count_first // 2
        else:
            axis, count_second = "gy", count_second // 2
        merge_plan.append((axis, bits[axis]))
        bits[axis] += 1
    return merge_plan


def staged(plan):
    stages, start, size = [], 0, 2
    while start < len(plan):
        stages.append(plan[start : start + size])
        start, size = start + size, 3
    return stages


def point_tables():
    index = np.arange(NODE)
    points = -np.cos(np.pi * index / (NODE - 1))
    weights = np.where(index % 2 == 0, 1.0, -1.0)
    weights[[0, NODE - 1]] *= 2.0
    eye = np.eye(NODE)
    matrix = weights[:, None] / weights[None, :] / (points[:, None] - points[None, :] + eye)
    matrix = matrix * (1.0 - eye)
    matrix = matrix - np.diag(matrix.sum(axis=1))
    both = np.concatenate([np.kron(matrix, eye).T, np.kron(eye, matrix).T], axis=1)
    both = both.astype(np.float32)
    high = both.astype(jnp.bfloat16)
    low = (both - high.astype(np.float32)).astype(jnp.bfloat16)
    facing = np.zeros((SQUARE, 2 * SQUARE), np.float32)
    last = NODE - 1
    for k in range(NODE):
        facing[last * NODE + k, k] = 1.0
        facing[k, last * NODE + k] = 1.0
        facing[k * NODE + last, SQUARE + k * NODE] = 1.0
        facing[k * NODE, SQUARE + k * NODE + last] = 1.0
    return np.concatenate([high, low, facing.astype(jnp.bfloat16)], axis=1)


def split(x):
    high = x.astype(BF16)
    return high, (x - high.astype(F32)).astype(BF16)


def dot(left, right):
    return jnp.dot(left, right, preferred_element_type=F32)


def dot_across(left, right):
    return lax.dot_general(left, right, (((1,), (1,)), ((), ())), preferred_element_type=F32)


def product(x, weight, dot=dot):
    high, low = weight
    rows = x.shape[0]
    if rows >= 64:
        x_high, x_low = split(x)
        return dot(x_high, high) + dot(x_low, high) + dot(x_high, low)
    rest = x - x.astype(BF16).astype(F32)
    both = jnp.concatenate([x, rest], axis=0).astype(BF16)
    out = dot(both, high) + dot(both, low)
    return out[:rows] + out[rows:]


def lanes(shape):
    return lax.broadcasted_iota(jnp.int32, shape, len(shape) - 1)


def left_half(shape):
    return lanes(shape) < shape[-1] // 2


def kernel(stages, leaf_side, tracer_count, *refs):
    names = ["u", "velocity", "inflow", "tables", "leaf_solve", "leaf_skeleton", "leaf_lift"]
    names += [a + "_" + b for a in ("merge", "parent", "sibling") for b in ("first", "second", "rest")]
    names += ["root_map"]
    hbm = dict(zip(names, refs[: len(names)]))
    out_ref = refs[len(names)]
    rest = refs[len(names) + 1 :]
    v = dict(zip(names, rest[: len(names)]))
    (
        load_sem, force, near, w_second, level_one, down_one, solved, t0_ref, t1_ref,
        up_high, up_low, par_high, par_low,
        send_x, send_y, halo_x, halo_y, halo_send, halo_recv, chain, fold_high, fold_low,
    ) = rest[len(names) : len(names) + 22]
    stage_refs = rest[len(names) + 22 :]
    T, L = tracer_count, leaf_side
    leaves = L * L
    rows = T * leaves

    loads = {}
    for k, name in enumerate(names):
        loads[name] = pltpu.make_async_copy(hbm[name], v[name], load_sem.at[k])
    order = ["u", "tables", "velocity", "inflow", "parent_rest", "root_map", "leaf_skeleton"]
    order += ["merge_first", "merge_second", "merge_rest", "leaf_solve"]
    order += ["sibling_first", "sibling_second", "sibling_rest"]
    order += ["parent_second", "parent_first", "leaf_lift"]
    for name in order:
        loads[name].start()

    place = {"gx": lax.axis_index("gx"), "gy": lax.axis_index("gy")}
    count = {"gx": lax.axis_size("gx"), "gy": lax.axis_size("gy")}
    bit_of = lambda axis, bit: lax.rem(place[axis] // (1 << bit), 2)

    def partner(stage, mask):
        target = dict(place)
        for k, (axis, bit) in enumerate(stage):
            if mask >> (len(stage) - 1 - k) & 1:
                target[axis] = target[axis] + (1 - 2 * bit_of(axis, bit)) * (1 << bit)
        return (target["gx"], target["gy"])

    barrier = pltpu.get_barrier_semaphore()
    expected = jnp.int32(0)
    for stage in stages:
        for mask in range(1, 1 << len(stage)):
            pl.semaphore_signal(barrier, inc=1, device_id=partner(stage, mask), device_id_type=MESH)
            expected = expected + 1
    has, beside = {}, {}
    for axis in ("gx", "gy"):
        for way in (-1, 1):
            spot = dict(place)
            spot[axis] = spot[axis] + way
            beside[axis, way] = (spot["gx"], spot["gy"])
            has[axis, way] = place[axis] > 0 if way < 0 else place[axis] < count[axis] - 1

            @pl.when(has[axis, way])
            def _(axis=axis, way=way):
                pl.semaphore_signal(barrier, inc=1, device_id=beside[axis, way], device_id_type=MESH)

            expected = expected + jnp.where(has[axis, way], 1, 0)

    loads["u"].wait()
    loads["tables"].wait()
    u = v["u"][...].astype(F32).reshape(rows, SQUARE)
    ub = u.astype(BF16)
    facing = dot(ub, v["tables"][:, 4 * SQUARE :])
    for c in range(4):
        near[c * rows : (c + 1) * rows, :] = facing[:, c * 128 : (c + 1) * 128]
    for t in range(T):
        base = t * leaves
        send_x[1, t * L : (t + 1) * L, :] = facing[base + leaves - L : base + leaves, :128]
        send_x[0, t * L : (t + 1) * L, :] = facing[base : base + L, 128:256]
    for k in range(2):
        for c in range(2):
            line = pl.ds((2 + c) * rows + k * (L - 1), T * L, stride=L)
            send_y[k, c * T * L : (c + 1) * T * L, :] = near[line, :]
    loads["parent_rest"].wait()
    loads["root_map"].wait()
    plan = [entry for stage in stages for entry in stage]
    bits = [bit_of(axis, bit) for axis, bit in plan]
    own_half = lambda k, w: jnp.where(bits[k] == 1, w[:, 128:], w[:, :128])
    own_parent = lambda k: own_half(k, v["parent_rest"][4 + k])
    previous = None
    for k in range(len(plan)):
        previous = own_parent(k) if k == 0 else product(own_parent(k), split(previous))
        chain[k] = previous
    chain[len(plan)] = product(v["root_map"][...], split(previous))
    for k in range(4):
        par_high[k], par_low[k] = split(v["parent_rest"][k])
    pl.semaphore_wait(barrier, expected)

    def halo_copy(axis, way):
        k = 0 if way < 0 else 1
        source, target = (send_x, halo_x) if axis == "gx" else (send_y, halo_y)
        slot = k + (0 if axis == "gx" else 2)
        return pltpu.make_async_remote_copy(
            src_ref=source.at[k],
            dst_ref=target.at[k],
            send_sem=halo_send.at[slot],
            recv_sem=halo_recv.at[slot],
            device_id=beside[axis, way],
            device_id_type=MESH,
        )

    sides = [("gy", -1), ("gy", 1), ("gx", -1), ("gx", 1)]
    for axis, way in sides:

        @pl.when(has[axis, way])
        def _(axis=axis, way=way):
            halo_copy(axis, way).start()

    loads["velocity"].wait()
    loads["inflow"].wait()
    own = lax.broadcasted_iota(jnp.int32, (leaves, L), 0) % L == lanes((leaves, L))

    def column(grid):
        wide = jnp.concatenate(
            [jnp.broadcast_to(grid[i : i + 1, :], (L, L)) for i in range(L)], axis=0
        )
        return jnp.sum(jnp.where(own, wide, 0.0), axis=1, keepdims=True)

    speed = [v["velocity"][k] for k in range(2)]
    strength = [
        column(v["inflow"][s].astype(F32) * (NODE * jnp.abs(speed[s // 2]))) for s in range(4)
    ]
    half = (leaves, SQUARE // 2)
    full = (leaves, SQUARE)
    weight_0 = jnp.where(lanes(half) < NODE, strength[0], 0.0)
    weight_1 = jnp.where(lanes(half) >= SQUARE // 2 - NODE, strength[1], 0.0)
    weight_2 = jnp.where(lanes(full) % NODE == 0, strength[2], 0.0)
    weight_3 = jnp.where(lanes(full) % NODE == NODE - 1, strength[3], 0.0)
    for k, weight in enumerate((weight_2, weight_3)):
        for c in range(2):
            at = (2 * k + c) * leaves
            w_second[at : at + leaves, :] = weight[:, c * 128 : (c + 1) * 128]
    keep = 1.0 - (jnp.concatenate([weight_0, weight_1], axis=1) + weight_2 + weight_3)
    spot = lax.broadcasted_iota(jnp.int32, full, 0) % L
    inner_2 = jnp.where(spot == 0, 0.0, weight_2)
    inner_3 = jnp.where(spot == L - 1, 0.0, weight_3)
    speed_0, speed_1 = column(speed[0]), column(speed[1])
    grads = dot(ub, v["tables"][:, : 2 * SQUARE]) + dot(ub, v["tables"][:, 2 * SQUARE : 4 * SQUARE])
    empty = jnp.zeros((L, SQUARE // 2), F32)
    for t in range(T):
        low, top = t * leaves, (t + 1) * leaves
        own_u = u[low:top]
        own_first = facing[low:top, :SQUARE]
        own_second = facing[low:top, SQUARE:].reshape(L, L, SQUARE)
        from_0 = jnp.concatenate([empty, own_first[: leaves - L, : SQUARE // 2]], axis=0)
        from_1 = jnp.concatenate([own_first[L:, SQUARE // 2 :], empty], axis=0)
        from_2 = pltpu.roll(own_second, 1, 1).reshape(leaves, SQUARE)
        from_3 = pltpu.roll(own_second, L - 1, 1).reshape(leaves, SQUARE)
        first = jnp.concatenate([weight_0 * from_0, weight_1 * from_1], axis=1)
        total = (
            keep * own_u
            - speed_0 * grads[low:top, :SQUARE]
            - speed_1 * grads[low:top, SQUARE:]
            + first
            + inner_2 * from_2
            + inner_3 * from_3
        )
        for c in range(2):
            force[c * rows + low : c * rows + top, :] = total[:, c * 128 : (c + 1) * 128]

    for name in ("leaf_skeleton", "merge_first", "merge_second", "merge_rest"):
        loads[name].wait()
    depth = v["merge_rest"].shape[0]
    for k in range(depth):
        up_high[k], up_low[k] = split(v["merge_rest"][k])
    up = lambda k: (up_high[k], up_low[k])
    twice = lambda w, axis: jnp.concatenate([w, w], axis=axis)
    w_skeleton = split(twice(v["leaf_skeleton"][...], 0))
    w_first = split(twice(v["merge_first"][...], 0))
    w_merge_second = split(v["merge_second"][...])

    for axis, way in sides:

        @pl.when(has[axis, way])
        def _(axis=axis, way=way):
            k = 0 if way < 0 else 1
            halo_copy(axis, way).wait_send()
            halo_copy(axis, -way).wait_recv()
            arrived = (halo_x if axis == "gx" else halo_y)[1 - k]
            if axis == "gx":
                edge = 0 if way < 0 else leaves - L
                weight = weight_0[:L] if way < 0 else weight_1[leaves - L :]
                for t in range(T):
                    start = k * rows + t * leaves + edge
                    at = slice(start, start + L)
                    force[at, :] = force[at, :] + weight * arrived[t * L : (t + 1) * L]
            else:
                edge = 0 if way < 0 else L - 1
                for c in range(2):
                    weight = w_second[pl.ds((2 * k + c) * leaves + edge, L, stride=L), :]
                    weight = jnp.concatenate([weight] * T, axis=0)
                    at = pl.ds(c * rows + edge, T * L, stride=L)
                    line = arrived[c * T * L : (c + 1) * T * L]
                    force[at, :] = force[at, :] + weight * line

    forcing = jnp.concatenate([force[:rows, :], force[rows:, :]], axis=1)
    skeleton = product(forcing, w_skeleton, dot_across).reshape(T, L // 2, 2, L, 128)
    pair = (T * leaves // 2, 128)
    cat_0 = jnp.where(
        left_half(pair), skeleton[:, :, 0].reshape(pair), skeleton[:, :, 1].reshape(pair)
    )
    level_one[...] = product(cat_0, w_first, dot_across)
    boxes = [
        (a + 2 * c, b + 2 * d) for a in range(2) for b in range(2) for c in range(2) for d in range(2)
    ]
    stride = leaves // 2
    at_box = lambda i, j: pl.ds(i * L + j, T, stride=stride)
    is_left = left_half((T, 128))
    cat_1 = jnp.concatenate(
        [
            jnp.where(is_left, level_one[at_box(i, 2 * j), :], level_one[at_box(i, 2 * j + 1), :])
            for i, j in boxes
        ],
        axis=0,
    )
    current = product(cat_1, w_merge_second)

    def joined(x):
        middle = x.shape[0] // 2
        return jnp.concatenate([x[:middle], x[middle:]], axis=1)

    cats = []
    for k in range(4):
        cats.append(joined(current))
        current = product(cats[-1], up(k))

    level = 4
    path = []
    for number, stage in enumerate(stages):
        pool, stage_send, stage_recv = stage_refs[3 * number : 3 * number + 3]
        slots = 1 << len(stage)
        own_slot = jnp.int32(0)
        for axis, bit in stage:
            own_slot = own_slot * 2 + bit_of(axis, bit)
        pool[own_slot] = current
        copies = [
            pltpu.make_async_remote_copy(
                src_ref=pool.at[own_slot],
                dst_ref=pool.at[own_slot],
                send_sem=stage_send.at[mask],
                recv_sem=stage_recv.at[mask],
                device_id=partner(stage, mask),
                device_id_type=MESH,
            )
            for mask in range(1, slots)
        ]
        for copy in reversed(copies):
            copy.start()
        if number == 0:
            for name in ("leaf_solve", "sibling_first", "sibling_second", "sibling_rest"):
                loads[name].wait()
            local_terms = [product(cats[k], split(v["sibling_rest"][k])) for k in range(4)]
            t1_ref[...] = product(cat_1, split(v["sibling_second"][...]))
            t0_ref[...] = product(cat_0, split(v["sibling_first"][...]))
        final = number == len(stages) - 1
        if final:
            first = len(plan) - len(stage)
            weights = chain[len(plan)]
            for k in reversed(range(first, len(plan))):
                groups = weights.shape[1] // 128
                weights = product(v["merge_rest"][4 + k], split(weights))
                sibling = own_half(k, v["sibling_rest"][4 + k])
                if k > 0:
                    sibling = product(sibling, split(chain[k - 1]))
                mine = jnp.int32(0)
                for later in range(k + 1, len(plan)):
                    mine = mine + bits[later] * (1 << (len(plan) - 1 - later))
                blocks = [
                    weights[:, g * 128 : (g + 1) * 128] + jnp.where(mine == g, sibling, 0.0)
                    for g in range(groups)
                ]
                weights = jnp.concatenate(
                    [x[:128] for x in blocks] + [x[128:] for x in blocks], axis=1
                )
            for g in range(slots):
                fold_high[g], fold_low[g] = split(weights[:, g * 128 : (g + 1) * 128])
            known = jnp.zeros((T, 128), F32)
            for k, term in enumerate(path):
                term = own_half(k, term)
                known = known + (product(term, split(chain[k - 1])) if k > 0 else term)
            solved[...] = product(forcing, split(v["leaf_solve"][...]))
            for name in ("parent_second", "parent_first", "leaf_lift"):
                loads[name].wait()
            w_parent_second = split(v["parent_second"][...])
            w_parent_first = split(twice(v["parent_first"][...], 0))
            w_lift = split(twice(v["leaf_lift"][...], 0))
        for copy in copies:
            copy.wait()
        if final:
            slabs = jnp.concatenate([pool[g] for g in range(slots)], axis=1)
            fold = [x[...].reshape(slots * 128, 128) for x in (fold_high, fold_low)]
            boundary = product(slabs, fold) + known
            break
        current = pool[...].reshape(slots * T, 128)
        for k, (axis, bit) in enumerate(stage):
            cat = joined(current)
            mine = cat
            for later_axis, later_bit in stage[k + 1 :]:
                middle = mine.shape[0] // 2
                mine = jnp.where(bit_of(later_axis, later_bit) == 1, mine[middle:], mine[:middle])
            path.append(product(mine, split(v["sibling_rest"][level])))
            current = product(cat, up(level))
            level += 1

    down = lambda k: (par_high[k], par_low[k])
    for k in reversed(range(4)):
        both = product(boundary, down(k)) + local_terms[k]
        boundary = jnp.concatenate([both[:, :128], both[:, 128:]], axis=0)
    both = product(boundary, w_parent_second) + t1_ref[...]
    for k, (i, j) in enumerate(boxes):
        one = both[k * T : (k + 1) * T]
        down_one[at_box(i, 2 * j), :] = jnp.where(is_left, one, 0.0)
        down_one[at_box(i, 2 * j + 1), :] = jnp.where(is_left, 0.0, one)
    both = product(down_one[...], w_parent_first) + t0_ref[...]
    split_left = left_half(pair)
    shape = (T, L // 2, 1, L, 128)
    leaf_boundary = jnp.concatenate(
        [
            jnp.where(split_left, both, 0.0).reshape(shape),
            jnp.where(split_left, 0.0, both).reshape(shape),
        ],
        axis=2,
    ).reshape(rows, 128)
    updated = solved[...] + product(leaf_boundary, w_lift)
    out_ref[...] = updated.reshape(out_ref.shape).astype(out_ref.dtype)


def local(tables, count_first, count_second, tracers, *operands):
    T, L = tracers.shape[0], tracers.shape[1]
    assert L == 8 and local_plan(L) == [1, 2] * 3
    stages = staged(cross_plan(count_first, count_second))
    rows = T * L * L
    args = [tracers, operands[0], operands[1], tables] + list(operands[2:])
    args[5], args[7] = args[5].T, args[7].T
    depth = operands[7].shape[0]
    vmem, dma = pltpu.VMEM, pltpu.SemaphoreType.DMA
    scratch = [vmem(a.shape, a.dtype) for a in args]
    scratch += [
        dma((len(args),)),
        vmem((2 * rows, 128), F32),
        vmem((4 * rows, 128), F32),
        vmem((4 * L * L, 128), F32),
        vmem((rows // 2, 128), F32),
        vmem((rows // 2, 128), F32),
        vmem((rows, SQUARE), F32),
        vmem((rows // 2, 128), F32),
        vmem((rows // 4, 128), F32),
        vmem((depth, 256, 128), BF16),
        vmem((depth, 256, 128), BF16),
        vmem((4, 128, 256), BF16),
        vmem((4, 128, 256), BF16),
        vmem((2, T * L, 128), F32),
        vmem((2, 2 * T * L, 128), F32),
        vmem((2, T * L, 128), F32),
        vmem((2, 2 * T * L, 128), F32),
        dma((4,)),
        dma((4,)),
        vmem((depth, 128, 128), F32),
        vmem((1 << len(stages[-1]), 128, 128), BF16),
        vmem((1 << len(stages[-1]), 128, 128), BF16),
    ]
    for stage in stages:
        slots = 1 << len(stage)
        scratch += [vmem((slots, T, 128), F32), dma((slots,)), dma((slots,))]
    return pl.pallas_call(
        functools.partial(kernel, stages, L, T),
        out_shape=jax.ShapeDtypeStruct(tracers.shape, tracers.dtype),
        in_specs=[pl.BlockSpec(memory_space=pl.ANY)] * len(args),
        out_specs=pl.BlockSpec(memory_space=pltpu.VMEM),
        scratch_shapes=scratch,
        compiler_params=pltpu.CompilerParams(
            collective_id=0, has_side_effects=True, vmem_limit_bytes=VMEM_LIMIT
        ),
    )(*[pltpu.with_memory_space_constraint(a, pltpu.HBM) for a in args])


def solution(mesh):
    tables = point_tables()
    split_both = P(None, "gx", "gy")
    in_specs = (P(None, "gx", "gy", None), split_both, split_both) + (P(),) * 13

    def body(*args):
        return local(
            jnp.asarray(tables), mesh.shape["gx"], mesh.shape["gy"], *args
        )

    return jax.shard_map(
        body,
        mesh=mesh,
        in_specs=in_specs,
        out_specs=P(None, "gx", "gy", None),
        check_vma=False,
    )
```

```python
import functools

import jax
import jax.numpy as jnp
import numpy as np
from jax import lax
from jax.experimental import pallas as pl
from jax.experimental.pallas import tpu as pltpu
from jax.sharding import PartitionSpec as P

NODE = 16
SQUARE = NODE * NODE
F32 = jnp.float32
BF16 = jnp.bfloat16
VMEM_LIMIT = 32 * 1024 * 1024
MESH = pl.DeviceIdType.MESH


def local_plan(leaf_side):
    merge_plan = []
    block_span = leaf_side
    while block_span > 1:
        merge_plan = merge_plan + [1, 2]
        block_span = block_span // 2
    return merge_plan


def cross_plan(count_first, count_second):
    merge_plan = []
    bits = {"gx": 0, "gy": 0}
    while count_first * count_second > 1:
        if count_first >= count_second:
            axis, count_first = "gx", count_first // 2
        else:
            axis, count_second = "gy", count_second // 2
        merge_plan.append((axis, bits[axis]))
        bits[axis] += 1
    return merge_plan


def staged(plan):
    stages, start, size = [], 0, 2
    while start < len(plan):
        stages.append(plan[start : start + size])
        start, size = start + size, 3
    return stages


def point_tables():
    index = np.arange(NODE)
    points = -np.cos(np.pi * index / (NODE - 1))
    weights = np.where(index % 2 == 0, 1.0, -1.0)
    weights[[0, NODE - 1]] *= 2.0
    eye = np.eye(NODE)
    matrix = weights[:, None] / weights[None, :] / (points[:, None] - points[None, :] + eye)
    matrix = matrix * (1.0 - eye)
    matrix = matrix - np.diag(matrix.sum(axis=1))
    both = np.concatenate([np.kron(matrix, eye).T, np.kron(eye, matrix).T], axis=1)
    both = both.astype(np.float32)
    high = both.astype(jnp.bfloat16)
    low = (both - high.astype(np.float32)).astype(jnp.bfloat16)
    facing = np.zeros((SQUARE, 2 * SQUARE), np.float32)
    last = NODE - 1
    for k in range(NODE):
        facing[last * NODE + k, k] = 1.0
        facing[k, last * NODE + k] = 1.0
        facing[k * NODE + last, SQUARE + k * NODE] = 1.0
        facing[k * NODE, SQUARE + k * NODE + last] = 1.0
    return np.concatenate([high, low, facing.astype(jnp.bfloat16)], axis=1)


def split(x):
    high = x.astype(BF16)
    return high, (x - high.astype(F32)).astype(BF16)


def dot(left, right):
    return jnp.dot(left, right, preferred_element_type=F32)


def dot_across(left, right):
    return lax.dot_general(left, right, (((1,), (1,)), ((), ())), preferred_element_type=F32)


def product(x, weight, dot=dot):
    high, low = weight
    rows = x.shape[0]
    if rows >= 64:
        x_high, x_low = split(x)
        return dot(x_high, high) + dot(x_low, high) + dot(x_high, low)
    rest = x - x.astype(BF16).astype(F32)
    both = jnp.concatenate([x, rest], axis=0).astype(BF16)
    out = dot(both, high) + dot(both, low)
    return out[:rows] + out[rows:]


def lanes(shape):
    return lax.broadcasted_iota(jnp.int32, shape, len(shape) - 1)


def left_half(shape):
    return lanes(shape) < shape[-1] // 2


def kernel(stages, leaf_side, tracer_count, *refs):
    names = ["u", "velocity", "inflow", "tables", "leaf_solve", "leaf_skeleton", "leaf_lift"]
    names += [a + "_" + b for a in ("merge", "parent", "sibling") for b in ("first", "second", "rest")]
    names += ["root_map"]
    hbm = dict(zip(names, refs[: len(names)]))
    out_ref = refs[len(names)]
    rest = refs[len(names) + 1 :]
    v = dict(zip(names, rest[: len(names)]))
    (
        load_sem, force, near, w_second, level_one, down_one, solved, t0_ref, t1_ref,
        up_high, up_low, par_high, par_low,
        send_x, send_y, halo_x, halo_y, halo_send, halo_recv, chain, fold_high, fold_low,
    ) = rest[len(names) : len(names) + 22]
    stage_refs = rest[len(names) + 22 :]
    T, L = tracer_count, leaf_side
    leaves = L * L
    rows = T * leaves

    loads = {}
    for k, name in enumerate(names):
        loads[name] = pltpu.make_async_copy(hbm[name], v[name], load_sem.at[k])
    order = ["u", "tables", "velocity", "inflow", "leaf_skeleton"]
    order += ["merge_first", "merge_second", "merge_rest", "leaf_solve"]
    order += ["sibling_first", "sibling_second", "sibling_rest", "parent_rest", "root_map"]
    order += ["parent_second", "parent_first", "leaf_lift"]
    for name in order:
        loads[name].start()

    place = {"gx": lax.axis_index("gx"), "gy": lax.axis_index("gy")}
    count = {"gx": lax.axis_size("gx"), "gy": lax.axis_size("gy")}
    bit_of = lambda axis, bit: lax.rem(place[axis] // (1 << bit), 2)

    def partner(stage, mask):
        target = dict(place)
        for k, (axis, bit) in enumerate(stage):
            if mask >> (len(stage) - 1 - k) & 1:
                target[axis] = target[axis] + (1 - 2 * bit_of(axis, bit)) * (1 << bit)
        return (target["gx"], target["gy"])

    barrier = pltpu.get_barrier_semaphore()
    expected = jnp.int32(0)
    for stage in stages:
        for mask in range(1, 1 << len(stage)):
            pl.semaphore_signal(barrier, inc=1, device_id=partner(stage, mask), device_id_type=MESH)
            expected = expected + 1
    has, beside = {}, {}
    for axis in ("gx", "gy"):
        for way in (-1, 1):
            spot = dict(place)
            spot[axis] = spot[axis] + way
            beside[axis, way] = (spot["gx"], spot["gy"])
            has[axis, way] = place[axis] > 0 if way < 0 else place[axis] < count[axis] - 1

            @pl.when(has[axis, way])
            def _(axis=axis, way=way):
                pl.semaphore_signal(barrier, inc=1, device_id=beside[axis, way], device_id_type=MESH)

            expected = expected + jnp.where(has[axis, way], 1, 0)

    loads["u"].wait()
    loads["tables"].wait()
    u = v["u"][...].astype(F32).reshape(rows, SQUARE)
    ub = u.astype(BF16)
    facing = dot(ub, v["tables"][:, 4 * SQUARE :])
    for c in range(4):
        near[c * rows : (c + 1) * rows, :] = facing[:, c * 128 : (c + 1) * 128]
    lines = lambda start, c: jnp.concatenate(
        [
            facing[t * leaves + start : t * leaves + start + L, c * 128 : (c + 1) * 128]
            for t in range(T)
        ],
        axis=0,
    )
    send_x[1] = lines(leaves - L, 0).astype(BF16)
    send_x[0] = lines(0, 1).astype(BF16)
    for k in range(2):
        parts = [
            near[pl.ds((2 + c) * rows + k * (L - 1), T * L, stride=L), :] for c in range(2)
        ]
        send_y[k] = (parts[0] + pltpu.roll(parts[1], 2, 1)).astype(BF16)
    pl.semaphore_wait(barrier, expected)

    def halo_copy(axis, way):
        k = 0 if way < 0 else 1
        source, target = (send_x, halo_x) if axis == "gx" else (send_y, halo_y)
        slot = k + (0 if axis == "gx" else 2)
        return pltpu.make_async_remote_copy(
            src_ref=source.at[k],
            dst_ref=target.at[k],
            send_sem=halo_send.at[slot],
            recv_sem=halo_recv.at[slot],
            device_id=beside[axis, way],
            device_id_type=MESH,
        )

    sides = [("gy", -1), ("gy", 1), ("gx", -1), ("gx", 1)]
    for axis, way in sides:

        @pl.when(has[axis, way])
        def _(axis=axis, way=way):
            halo_copy(axis, way).start()

    loads["velocity"].wait()
    loads["inflow"].wait()
    own = lax.broadcasted_iota(jnp.int32, (leaves, L), 0) % L == lanes((leaves, L))

    def column(grid):
        wide = jnp.concatenate(
            [jnp.broadcast_to(grid[i : i + 1, :], (L, L)) for i in range(L)], axis=0
        )
        return jnp.sum(jnp.where(own, wide, 0.0), axis=1, keepdims=True)

    speed = [v["velocity"][k] for k in range(2)]
    strength = [
        column(v["inflow"][s].astype(F32) * (NODE * jnp.abs(speed[s // 2]))) for s in range(4)
    ]
    half = (leaves, SQUARE // 2)
    full = (leaves, SQUARE)
    weight_0 = jnp.where(lanes(half) < NODE, strength[0], 0.0)
    weight_1 = jnp.where(lanes(half) >= SQUARE // 2 - NODE, strength[1], 0.0)
    weight_2 = jnp.where(lanes(full) % NODE == 0, strength[2], 0.0)
    weight_3 = jnp.where(lanes(full) % NODE == NODE - 1, strength[3], 0.0)
    for k, weight in enumerate((weight_2, weight_3)):
        for c in range(2):
            at = (2 * k + c) * leaves
            w_second[at : at + leaves, :] = weight[:, c * 128 : (c + 1) * 128]
    keep = 1.0 - (jnp.concatenate([weight_0, weight_1], axis=1) + weight_2 + weight_3)
    spot = lax.broadcasted_iota(jnp.int32, full, 0) % L
    inner_2 = jnp.where(spot == 0, 0.0, weight_2)
    inner_3 = jnp.where(spot == L - 1, 0.0, weight_3)
    speed_0, speed_1 = column(speed[0]), column(speed[1])
    grads = dot(ub, v["tables"][:, : 2 * SQUARE]) + dot(ub, v["tables"][:, 2 * SQUARE : 4 * SQUARE])
    empty = jnp.zeros((L, SQUARE // 2), F32)
    for t in range(T):
        low, top = t * leaves, (t + 1) * leaves
        own_u = u[low:top]
        own_first = facing[low:top, :SQUARE]
        own_second = facing[low:top, SQUARE:].reshape(L, L, SQUARE)
        from_0 = jnp.concatenate([empty, own_first[: leaves - L, : SQUARE // 2]], axis=0)
        from_1 = jnp.concatenate([own_first[L:, SQUARE // 2 :], empty], axis=0)
        from_2 = pltpu.roll(own_second, 1, 1).reshape(leaves, SQUARE)
        from_3 = pltpu.roll(own_second, L - 1, 1).reshape(leaves, SQUARE)
        first = jnp.concatenate([weight_0 * from_0, weight_1 * from_1], axis=1)
        total = (
            keep * own_u
            - speed_0 * grads[low:top, :SQUARE]
            - speed_1 * grads[low:top, SQUARE:]
            + first
            + inner_2 * from_2
            + inner_3 * from_3
        )
        for c in range(2):
            force[c * rows + low : c * rows + top, :] = total[:, c * 128 : (c + 1) * 128]

    for name in ("leaf_skeleton", "merge_first", "merge_second", "merge_rest"):
        loads[name].wait()
    depth = v["merge_rest"].shape[0]
    for k in range(depth):
        up_high[k], up_low[k] = split(v["merge_rest"][k])
    up = lambda k: (up_high[k], up_low[k])
    twice = lambda w, axis: jnp.concatenate([w, w], axis=axis)
    w_skeleton = split(twice(v["leaf_skeleton"][...], 0))
    w_first = split(twice(v["merge_first"][...], 0))
    w_merge_second = split(v["merge_second"][...])

    for axis, way in sides:

        @pl.when(has[axis, way])
        def _(axis=axis, way=way):
            k = 0 if way < 0 else 1
            halo_copy(axis, way).wait_send()
            halo_copy(axis, -way).wait_recv()
            arrived = (halo_x if axis == "gx" else halo_y)[1 - k].astype(F32)
            if axis == "gx":
                edge = 0 if way < 0 else leaves - L
                weight = weight_0[:L] if way < 0 else weight_1[leaves - L :]
                for t in range(T):
                    start = k * rows + t * leaves + edge
                    at = slice(start, start + L)
                    force[at, :] = force[at, :] + weight * arrived[t * L : (t + 1) * L]
            else:
                edge = 0 if way < 0 else L - 1
                for c in range(2):
                    weight = w_second[pl.ds((2 * k + c) * leaves + edge, L, stride=L), :]
                    weight = jnp.concatenate([weight] * T, axis=0)
                    at = pl.ds(c * rows + edge, T * L, stride=L)
                    line = arrived if c == 0 else pltpu.roll(arrived, 126, 1)
                    force[at, :] = force[at, :] + weight * line

    forcing = jnp.concatenate([force[:rows, :], force[rows:, :]], axis=1)
    skeleton = product(forcing, w_skeleton, dot_across).reshape(T, L // 2, 2, L, 128)
    pair = (T * leaves // 2, 128)
    cat_0 = jnp.where(
        left_half(pair), skeleton[:, :, 0].reshape(pair), skeleton[:, :, 1].reshape(pair)
    )
    level_one[...] = product(cat_0, w_first, dot_across)
    boxes = [
        (a + 2 * c, b + 2 * d) for a in range(2) for b in range(2) for c in range(2) for d in range(2)
    ]
    stride = leaves // 2
    at_box = lambda i, j: pl.ds(i * L + j, T, stride=stride)
    is_left = left_half((T, 128))
    cat_1 = jnp.concatenate(
        [
            jnp.where(is_left, level_one[at_box(i, 2 * j), :], level_one[at_box(i, 2 * j + 1), :])
            for i, j in boxes
        ],
        axis=0,
    )
    current = product(cat_1, w_merge_second)

    def joined(x):
        middle = x.shape[0] // 2
        return jnp.concatenate([x[:middle], x[middle:]], axis=1)

    cats = []
    for k in range(4):
        cats.append(joined(current))
        current = product(cats[-1], up(k))

    level = 4
    plan = [entry for stage in stages for entry in stage]
    bits = [bit_of(axis, bit) for axis, bit in plan]
    own_half = lambda k, w: jnp.where(bits[k] == 1, w[:, 128:], w[:, :128])
    own_parent = lambda k: own_half(k, v["parent_rest"][4 + k])
    path = []
    for number, stage in enumerate(stages):
        pool, stage_send, stage_recv = stage_refs[3 * number : 3 * number + 3]
        slots = 1 << len(stage)
        own_slot = jnp.int32(0)
        for axis, bit in stage:
            own_slot = own_slot * 2 + bit_of(axis, bit)
        pool[own_slot] = current
        copies = [
            pltpu.make_async_remote_copy(
                src_ref=pool.at[own_slot],
                dst_ref=pool.at[own_slot],
                send_sem=stage_send.at[mask],
                recv_sem=stage_recv.at[mask],
                device_id=partner(stage, mask),
                device_id_type=MESH,
            )
            for mask in range(1, slots)
        ]
        for copy in reversed(copies):
            copy.start()
        if number == 0:
            for name in ("leaf_solve", "sibling_first", "sibling_second", "sibling_rest"):
                loads[name].wait()
            local_terms = [product(cats[k], split(v["sibling_rest"][k])) for k in range(4)]
            t1_ref[...] = product(cat_1, split(v["sibling_second"][...]))
            t0_ref[...] = product(cat_0, split(v["sibling_first"][...]))
            loads["parent_rest"].wait()
            loads["root_map"].wait()
            previous = None
            for k in range(len(plan)):
                previous = own_parent(k) if k == 0 else product(own_parent(k), split(previous))
                chain[k] = previous
            chain[len(plan)] = product(v["root_map"][...], split(previous))
            for k in range(4):
                par_high[k], par_low[k] = split(v["parent_rest"][k])
        final = number == len(stages) - 1
        if final:
            first = len(plan) - len(stage)
            weights = chain[len(plan)]
            for k in reversed(range(first, len(plan))):
                groups = weights.shape[1] // 128
                weights = product(v["merge_rest"][4 + k], split(weights))
                sibling = own_half(k, v["sibling_rest"][4 + k])
                if k > 0:
                    sibling = product(sibling, split(chain[k - 1]))
                mine = jnp.int32(0)
                for later in range(k + 1, len(plan)):
                    mine = mine + bits[later] * (1 << (len(plan) - 1 - later))
                blocks = [
                    weights[:, g * 128 : (g + 1) * 128] + jnp.where(mine == g, sibling, 0.0)
                    for g in range(groups)
                ]
                weights = jnp.concatenate(
                    [x[:128] for x in blocks] + [x[128:] for x in blocks], axis=1
                )
            for g in range(slots):
                fold_high[g], fold_low[g] = split(weights[:, g * 128 : (g + 1) * 128])
            known = jnp.zeros((T, 128), F32)
            for k, term in enumerate(path):
                term = own_half(k, term)
                known = known + (product(term, split(chain[k - 1])) if k > 0 else term)
            solved[...] = product(forcing, split(v["leaf_solve"][...]))
            for name in ("parent_second", "parent_first", "leaf_lift"):
                loads[name].wait()
            w_parent_second = split(v["parent_second"][...])
            w_parent_first = split(twice(v["parent_first"][...], 0))
            w_lift = split(twice(v["leaf_lift"][...], 0))
        for copy in copies:
            copy.wait()
        if final:
            slabs = jnp.concatenate([pool[g] for g in range(slots)], axis=1)
            fold = [x[...].reshape(slots * 128, 128) for x in (fold_high, fold_low)]
            boundary = product(slabs, fold) + known
            break
        current = pool[...].reshape(slots * T, 128)
        for k, (axis, bit) in enumerate(stage):
            cat = joined(current)
            mine = cat
            for later_axis, later_bit in stage[k + 1 :]:
                middle = mine.shape[0] // 2
                mine = jnp.where(bit_of(later_axis, later_bit) == 1, mine[middle:], mine[:middle])
            path.append(product(mine, split(v["sibling_rest"][level])))
            current = product(cat, up(level))
            level += 1

    down = lambda k: (par_high[k], par_low[k])
    for k in reversed(range(4)):
        both = product(boundary, down(k)) + local_terms[k]
        boundary = jnp.concatenate([both[:, :128], both[:, 128:]], axis=0)
    both = product(boundary, w_parent_second) + t1_ref[...]
    for k, (i, j) in enumerate(boxes):
        one = both[k * T : (k + 1) * T]
        down_one[at_box(i, 2 * j), :] = jnp.where(is_left, one, 0.0)
        down_one[at_box(i, 2 * j + 1), :] = jnp.where(is_left, 0.0, one)
    both = product(down_one[...], w_parent_first) + t0_ref[...]
    split_left = left_half(pair)
    shape = (T, L // 2, 1, L, 128)
    leaf_boundary = jnp.concatenate(
        [
            jnp.where(split_left, both, 0.0).reshape(shape),
            jnp.where(split_left, 0.0, both).reshape(shape),
        ],
        axis=2,
    ).reshape(rows, 128)
    updated = solved[...] + product(leaf_boundary, w_lift)
    out_ref[...] = updated.reshape(out_ref.shape).astype(out_ref.dtype)


def local(tables, count_first, count_second, tracers, *operands):
    T, L = tracers.shape[0], tracers.shape[1]
    assert L == 8 and local_plan(L) == [1, 2] * 3
    stages = staged(cross_plan(count_first, count_second))
    rows = T * L * L
    args = [tracers, operands[0], operands[1], tables] + list(operands[2:])
    args[5], args[7] = args[5].T, args[7].T
    depth = operands[7].shape[0]
    vmem, dma = pltpu.VMEM, pltpu.SemaphoreType.DMA
    scratch = [vmem(a.shape, a.dtype) for a in args]
    scratch += [
        dma((len(args),)),
        vmem((2 * rows, 128), F32),
        vmem((4 * rows, 128), F32),
        vmem((4 * L * L, 128), F32),
        vmem((rows // 2, 128), F32),
        vmem((rows // 2, 128), F32),
        vmem((rows, SQUARE), F32),
        vmem((rows // 2, 128), F32),
        vmem((rows // 4, 128), F32),
        vmem((depth, 256, 128), BF16),
        vmem((depth, 256, 128), BF16),
        vmem((4, 128, 256), BF16),
        vmem((4, 128, 256), BF16),
        vmem((2, T * L, 128), BF16),
        vmem((2, T * L, 128), BF16),
        vmem((2, T * L, 128), BF16),
        vmem((2, T * L, 128), BF16),
        dma((4,)),
        dma((4,)),
        vmem((depth, 128, 128), F32),
        vmem((1 << len(stages[-1]), 128, 128), BF16),
        vmem((1 << len(stages[-1]), 128, 128), BF16),
    ]
    for stage in stages:
        slots = 1 << len(stage)
        scratch += [vmem((slots, T, 128), F32), dma((slots,)), dma((slots,))]
    return pl.pallas_call(
        functools.partial(kernel, stages, L, T),
        out_shape=jax.ShapeDtypeStruct(tracers.shape, tracers.dtype),
        in_specs=[pl.BlockSpec(memory_space=pl.ANY)] * len(args),
        out_specs=pl.BlockSpec(memory_space=pltpu.VMEM),
        scratch_shapes=scratch,
        compiler_params=pltpu.CompilerParams(
            collective_id=0, has_side_effects=True, vmem_limit_bytes=VMEM_LIMIT
        ),
    )(*[pltpu.with_memory_space_constraint(a, pltpu.HBM) for a in args])


def solution(mesh):
    tables = point_tables()
    split_both = P(None, "gx", "gy")
    in_specs = (P(None, "gx", "gy", None), split_both, split_both) + (P(),) * 13

    def body(*args):
        return local(
            jnp.asarray(tables), mesh.shape["gx"], mesh.shape["gy"], *args
        )

    return jax.shard_map(
        body,
        mesh=mesh,
        in_specs=in_specs,
        out_specs=P(None, "gx", "gy", None),
        check_vma=False,
    )
```
